32 devices in a mesh: chan: 16 (over z, x, core), pix: 2 (over y).
Axes of the slice: x: 2, y: 2, z: 4, core: 2. Of those that a mesh axis runs over, the one named last changes fastest.
Arguments:
- cube: float32 [512, 16384], P('pix', 'chan'), as said below
- windows: int32 [8], replicated, may hold values from 1 to 1024, as said below
- mask: int32 [16384], replicated, may hold values from 0 to 1, as said below
Outputs:
- subtracted: float32 [512, 16384], P('pix', 'chan')
The draws below stay inside these ranges and needn't reach their ends.
Inputs may be any that keep to these rules, and one draw needn't show every extreme that they name: windows[0] is 1024 and windows[7] is 1; for 0 < k < 7, windows[k] is at most 1024 halved k times (rounded down) and more than three quarters of that, but 1 or more. `mask`: zero on 8 disjoint ranges of 256 to 512 channels each, one elsewhere; the k-th range lies inside channels k * 2048 to (k + 1) * 2048 - 1, at least 512 channels from that slot's edges, and at least 1024 channels from either end of the band. `cube`: each spectrum is a smooth continuum of low order plus noise whose level varies from channel to channel.
All inputs are finite; a program needn't handle non-finite values.
Results may differ from the reference program's by a relative error of at most 0.00021.
Values sent between devices are 32-bit elements; how exact they have to be, the bound alone decides.
A program may use at most 64 MiB of HBM per device.

```python
import jax
import jax.numpy as jnp
from jax import lax

NC = 16384
TERMS = 16
PASSES = 8
WMAX = 1024
PIX_DEV = 16
NPIX = 512


def draw_cube(key, part):
    keys = jax.random.split(key, 4)
    xvals = (2.0 * jnp.arange(NC).astype(jnp.float32) + 1.0) / NC - 1.0
    table = jnp.stack([jnp.ones_like(xvals), xvals, 1.5 * xvals * xvals - 0.5, 2.5 * xvals ** 3 - 1.5 * xvals], axis=0)
    level = jax.random.uniform(keys[0], (NPIX, 1), jnp.float32, 3.0, 10.0)
    slopes = jax.random.normal(keys[1], (NPIX, 3), jnp.float32)
    coefs = jnp.concatenate([level, slopes], axis=1)
    continuum = coefs @ table
    chan_scale = jnp.exp(jax.random.uniform(keys[2], (1, NC), jnp.float32, jnp.log(0.5), jnp.log(2.0)))
    noise = jax.random.normal(keys[3], (NPIX, NC), jnp.float32)
    return (continuum + noise * chan_scale).astype(jnp.float32)


def draw_windows(key, part):
    steps = jnp.arange(PASSES, dtype=jnp.int32)
    base = jnp.right_shift(jnp.int32(WMAX), steps)
    spread = jnp.maximum(1, jnp.right_shift(jnp.int32(WMAX), steps + 2))
    jitter = jax.random.randint(key, (PASSES,), 0, spread, jnp.int32)
    widths = jnp.maximum(1, base - jitter)
    widths = widths.at[0].set(WMAX)
    widths = widths.at[PASSES - 1].set(1)
    return widths.astype(jnp.int32)


def draw_mask(key, part):
    keys = jax.random.split(key, 2)
    slot = NC // 8
    slots = jnp.arange(8, dtype=jnp.int32)[:, None]
    spans = jax.random.randint(keys[0], (8, 1), NC // 64, NC // 32 + 1, jnp.int32)
    low_margin = jnp.where(slots == 0, NC // 16, NC // 32).astype(jnp.int32)
    high_margin = jnp.where(slots == 7, NC // 16, NC // 32).astype(jnp.int32)
    room = slot - low_margin - high_margin - spans + 1
    offsets = jax.random.randint(keys[1], (8, 1), 0, 1 << 20, jnp.int32) % room
    starts = slots * slot + low_margin + offsets
    column = jnp.arange(NC, dtype=jnp.int32)[None, :]
    inside = (column >= starts) & (column < starts + spans)
    return (1 - jnp.any(inside, axis=0).astype(jnp.int32)).astype(jnp.int32)


def setup_inputs(seed: int = 0) -> dict:
    key_list = jax.random.split(jax.random.key(seed), 4)
    cube = draw_cube(jax.random.fold_in(key_list[3], 71), 0)
    windows = draw_windows(jax.random.fold_in(key_list[3], 71), 0)
    mask = draw_mask(jax.random.fold_in(key_list[3], 71), 0)
    return {"cube": cube, "windows": windows, "mask": mask}


def legendre(xvals):
    rows = [jnp.ones_like(xvals), xvals]
    for order in range(1, TERMS - 1):
        rows.append(((2.0 * order + 1.0) * xvals * rows[order] - order * rows[order - 1]) / (order + 1.0))
    return jnp.stack(rows[:TERMS], axis=0)

def snip(spectra, windows):
    count = spectra.shape[1]
    column = lax.broadcasted_iota(jnp.int32, (1, count), 1)
    for step in range(PASSES):
        width = windows[step]
        padded = jnp.pad(spectra, ((0, 0), (WMAX, WMAX)))
        lower = lax.dynamic_slice_in_dim(padded, (WMAX - width).astype(jnp.int32), count, 1)
        upper = lax.dynamic_slice_in_dim(padded, (WMAX + width).astype(jnp.int32), count, 1)
        inside = (column >= width) & (column < count - width)
        spectra = jnp.where(inside, jnp.minimum(spectra, 0.5 * (lower + upper)), spectra)
    return spectra

def reference(cube, windows, mask):
    xvals = (2.0 * jnp.arange(NC, dtype=jnp.int32).astype(jnp.float32) + 1.0) / NC - 1.0
    table = legendre(xvals)
    weighted = table * mask.astype(jnp.float32)[None, :]
    gram = jnp.dot(weighted, table.T, precision=lax.Precision.HIGHEST)
    factor = jnp.linalg.cholesky(gram)

    def one_block(block):
        baseline = snip(block, windows)
        rhs = jnp.dot(weighted, baseline.T, precision=lax.Precision.HIGHEST)
        middle = lax.linalg.triangular_solve(factor, rhs, left_side=True, lower=True)
        coef = lax.linalg.triangular_solve(factor, middle, left_side=True, lower=True, transpose_a=True)
        return block - jnp.dot(coef.T, table, precision=lax.Precision.HIGHEST)
    blocks = cube.reshape(NPIX // PIX_DEV, PIX_DEV, NC)
    return lax.map(one_block, blocks).reshape(NPIX, NC)
```

```python
import functools
import math

import jax
import jax.numpy as jnp
import numpy as np
from jax import lax
from jax.experimental import pallas as pl
from jax.experimental.pallas import tpu as pltpu
from jax.sharding import PartitionSpec as P

TERMS = 16
PASSES = 8
WMAX = 1024
HALO = 2 * WMAX
LANES = 128
BLOCK = 16
CHUNKS = 4
MESH = pl.DeviceIdType.MESH
F32 = jnp.float32
BF16 = jnp.bfloat16


def linearization():
    def a(r):
        return math.comb(2 * r, r) / 2.0**r

    out = np.zeros((2 * TERMS - 1, TERMS, TERMS))
    for n in range(TERMS):
        for m in range(TERMS):
            for r in range(min(n, m) + 1):
                k = n + m - 2 * r
                out[k, n, m] = (
                    a(r) * a(n - r) * a(m - r) / a(n + m - r)
                    * (2 * k + 1) / (2 * n + 2 * m - 2 * r + 1)
                )
    return out.astype(np.float32)


def next_legendre(order, xvals, here, before):
    return ((2.0 * order + 1.0) * xvals * here - order * before) * (1.0 / (order + 1.0))


def split3(v):
    hi = v.astype(BF16)
    rest = v - hi.astype(F32)
    mid = rest.astype(BF16)
    lo = (rest - mid.astype(F32)).astype(BF16)
    return hi, mid, lo


def kernel(
    n_chan, group, total,
    windows, cube, mask_sq, mask_row, lin,
    out,
    held, raw, ping, pong, fit_hi, fit_lo, table, w3, sums,
    load_sem, own_sem, send_sem, hop_sem, recv_sem, up_sem, down_sem, sum_send, sum_recv,
):
    pix, ch = held.shape
    rows = raw.shape[0]
    slab_ch = group * ch
    tiles = slab_ch // LANES
    slabs = n_chan // group
    part = rows // CHUNKS
    me = lax.axis_index("chan")
    slab = me // group
    g = lax.rem(me, group)
    own_col = pl.multiple_of(HALO + g * ch, LANES)

    def peer(b):
        return {"chan": slab * group + b}

    load = pltpu.make_async_copy(cube, held, load_sem)
    load.start()
    barrier = pltpu.get_barrier_semaphore()
    for k in range(1, n_chan):
        pl.semaphore_signal(
            barrier, inc=1, device_id={"chan": lax.rem(me + k, n_chan)}, device_id_type=MESH
        )

    @pl.when(slab == 0)
    def _():
        raw[:, 0:HALO] = jnp.full((rows, HALO), jnp.inf, F32)

    @pl.when(slab == slabs - 1)
    def _():
        raw[:, HALO + slab_ch :] = jnp.full((rows, HALO), jnp.inf, F32)

    load.wait()
    own_rows = pl.multiple_of(g * rows, 8)
    own = pltpu.make_async_copy(
        held.at[pl.ds(own_rows, rows), :], raw.at[:, pl.ds(own_col, ch)], own_sem
    )
    own.start()
    pl.semaphore_wait(barrier, n_chan - 1)

    def chunk(c):
        return pl.ds(c * part, part)

    def slab_send(c, b):
        return pltpu.make_async_remote_copy(
            src_ref=held.at[pl.ds(b * rows + c * part, part), :],
            dst_ref=raw.at[chunk(c), pl.ds(own_col, ch)],
            send_sem=send_sem, recv_sem=recv_sem.at[c, g],
            device_id=peer(b), device_id_type=MESH,
        )

    def slab_recv(c, b):
        return pltpu.make_async_remote_copy(
            src_ref=held.at[pl.ds(c * part, part), :],
            dst_ref=raw.at[chunk(c), pl.ds(HALO + b * ch, ch)],
            send_sem=send_sem, recv_sem=recv_sem.at[c, b],
            device_id=peer(b), device_id_type=MESH,
        )

    def hop(c, b, up, from_own):
        if up:
            col = b * ch - (slab_ch - HALO)
            sem, to = up_sem.at[c], me + group
        else:
            col = HALO + slab_ch + b * ch
            sem, to = down_sem.at[c], me - group
        if from_own:
            src = held.at[pl.ds(pl.multiple_of(own_rows + c * part, 8), part), :]
        else:
            src = raw.at[chunk(c), pl.ds(HALO + b * ch, ch)]
        return pltpu.make_async_remote_copy(
            src_ref=src, dst_ref=raw.at[chunk(c), pl.ds(col, ch)],
            send_sem=hop_sem.at[0 if up else 1], recv_sem=sem,
            device_id={"chan": to}, device_id_type=MESH,
        )

    def goes_up(b):
        return b * ch >= slab_ch - HALO

    def goes_down(b):
        return b * ch < HALO

    def own_hops(c):
        for b in range(group):
            if goes_up(b):
                @pl.when((g == b) & (slab < slabs - 1))
                def _():
                    hop(c, b, True, True).start()
            if goes_down(b):
                @pl.when((g == b) & (slab > 0))
                def _():
                    hop(c, b, False, True).start()

    def forward(c):
        for b in range(group):
            @pl.when(g != b)
            def _():
                slab_recv(c, b).wait_recv()
                if goes_up(b):
                    @pl.when(slab < slabs - 1)
                    def _():
                        hop(c, b, True, False).start()
                if goes_down(b):
                    @pl.when(slab > 0)
                    def _():
                        hop(c, b, False, False).start()

    def halo_wait(c):
        def arrived(col, sem):
            return pltpu.make_async_remote_copy(
                src_ref=raw.at[chunk(c), pl.ds(col, HALO)],
                dst_ref=raw.at[chunk(c), pl.ds(col, HALO)],
                send_sem=hop_sem.at[0], recv_sem=sem,
                device_id={"chan": me}, device_id_type=MESH,
            )

        @pl.when(slab > 0)
        def _():
            arrived(0, up_sem.at[c]).wait_recv()

        @pl.when(slab < slabs - 1)
        def _():
            arrived(HALO + slab_ch, down_sem.at[c]).wait_recv()

    for c in range(CHUNKS):
        for b in range(group):
            @pl.when(g != b)
            def _():
                slab_send(c, b).start()
        own_hops(c)

    shape = mask_sq.shape
    index = lax.broadcasted_iota(jnp.int32, shape, 0) * shape[1] + lax.broadcasted_iota(
        jnp.int32, shape, 1
    )
    xvals = (2.0 * index.astype(F32) + 1.0) * (1.0 / total) - 1.0
    keep = mask_sq[...].astype(F32)
    here, before = jnp.ones_like(xvals), jnp.zeros_like(xvals)
    gram = jnp.zeros((TERMS, TERMS), F32)
    for k in range(2 * TERMS - 1):
        moment = jnp.sum(here * keep, axis=0, keepdims=True)
        moment = jnp.sum(moment, axis=1, keepdims=True)
        gram = gram + moment * lin[k]
        here, before = next_legendre(k, xvals, here, before), here

    row_id = lax.broadcasted_iota(jnp.int32, (TERMS, 2 * TERMS), 0)
    col_id = lax.broadcasted_iota(jnp.int32, (TERMS, 2 * TERMS), 1)
    eye = jnp.where(row_id + TERMS == col_id, 1.0, 0.0).astype(F32)
    aug = eye + jnp.concatenate([gram, jnp.zeros_like(gram)], axis=1)
    for p in range(TERMS):
        lead = aug[p : p + 1, :] / aug[p : p + 1, p : p + 1]
        aug = jnp.where(row_id == p, lead, aug - aug[:, p : p + 1] * lead)
    inverse = aug[:, TERMS:]

    forward(0)

    step = min(1024, slab_ch)
    base = slab * slab_ch
    for s in range(0, slab_ch, step):
        lane = lax.broadcasted_iota(jnp.int32, (1, step), 1)
        x_s = (2.0 * (base + s + lane).astype(F32) + 1.0) * (1.0 / total) - 1.0
        here, before = jnp.ones_like(x_s), jnp.zeros_like(x_s)
        for n in range(TERMS):
            table[n : n + 1, s : s + step] = here
            here, before = next_legendre(n, x_s, here, before), here
        keep_s = mask_row[:, pl.ds(pl.multiple_of(base + s, LANES), step)].astype(F32)
        hi, mid, lo = split3(table[:, s : s + step] * keep_s)
        w3[0:TERMS, s : s + step] = hi
        w3[TERMS : 2 * TERMS, s : s + step] = mid
        w3[2 * TERMS :, s : s + step] = lo

    forward(1)

    own.wait()
    lane = lax.broadcasted_iota(jnp.int32, (BLOCK, LANES), 1)
    edge = HALO // LANES

    def snip(start):
        r = pl.ds(start, BLOCK)

        def at(ref, t):
            return ref[:, (t + edge) * LANES : (t + edge + 1) * LANES]

        def put(ref, t, v):
            ref[:, (t + edge) * LANES : (t + edge + 1) * LANES] = v

        def first(t):
            return raw[r, (t + edge) * LANES : (t + edge + 1) * LANES]

        far = WMAX // LANES
        for t in range(-far, tiles + far):
            put(ping, t, jnp.minimum(first(t), 0.5 * (first(t - far) + first(t + far))))
        src, dst = ping, pong
        for k in range(1, PASSES):
            bound = max(LANES, WMAX >> k)
            b = bound // LANES
            d = bound - windows[k]
            back = lax.rem(LANES - d, LANES)
            low_here = lane < LANES - d
            high_here = lane >= d
            reach = 0 if k == PASSES - 1 else b
            left = {}
            right = {}
            for t in range(-reach, tiles + reach):
                for u in (t - b, t - b + 1):
                    if u not in left:
                        left[u] = pltpu.roll(at(src, u), back, 1)
                for u in (t + b - 1, t + b):
                    if u not in right:
                        right[u] = pltpu.roll(at(src, u), d, 1)
                lower = jnp.where(low_here, left[t - b], left[t - b + 1])
                upper = jnp.where(high_here, right[t + b], right[t + b - 1])
                v = jnp.minimum(at(src, t), 0.5 * (lower + upper))
                if k < PASSES - 1:
                    put(dst, t, v)
                else:
                    cols = slice(t * LANES, (t + 1) * LANES)
                    hi = v.astype(BF16)
                    fit_hi[r, cols] = hi
                    fit_lo[r, cols] = (v - hi.astype(F32)).astype(BF16)
            src, dst = dst, src

    def process(c):
        halo_wait(c)
        blocks = part // BLOCK
        if blocks == 1:
            snip(c * part)
        else:
            def body(i, carry):
                snip(pl.multiple_of(c * part + i * BLOCK, BLOCK))
                return carry
            lax.fori_loop(0, blocks, body, 0)

    for c in range(CHUNKS):
        if c + 2 < CHUNKS:
            forward(c + 2)
        process(c)

    dims = (((1,), (1,)), ((), ()))
    rhs3 = lax.dot_general(w3[...], fit_hi[...], dims, preferred_element_type=F32)
    rhs3 = rhs3 + lax.dot_general(w3[...], fit_lo[...], dims, preferred_element_type=F32)
    rhs = rhs3[0:TERMS] + (rhs3[TERMS : 2 * TERMS] + rhs3[2 * TERMS :])
    fold = sums.shape[2] // rows
    high = TERMS // fold
    packed = jnp.concatenate([rhs[i * high : (i + 1) * high] for i in range(fold)], axis=1)
    sums[me] = packed

    def sum_copy(k):
        return pltpu.make_async_remote_copy(
            src_ref=sums.at[me], dst_ref=sums.at[me],
            send_sem=sum_send, recv_sem=sum_recv,
            device_id={"chan": lax.rem(me + k, n_chan)}, device_id_type=MESH,
        )

    for k in range(1, n_chan):
        sum_copy(k).start()

    t_own = table[:, pl.ds(pl.multiple_of(g * ch, LANES), ch)]
    shaped = jnp.zeros_like(t_own)
    for m in range(TERMS):
        shaped = shaped + inverse[:, m : m + 1] * t_own[m : m + 1, :]
    a_hi, a_mid, a_lo = split3(shaped)
    zero = jnp.zeros_like(a_hi)
    right_side = jnp.concatenate([a_hi, a_mid, a_hi, a_lo, a_hi, a_mid, zero, zero], axis=0)

    def sent(ref, sem):
        return pltpu.make_async_remote_copy(
            src_ref=ref, dst_ref=ref, send_sem=sem, recv_sem=own_sem,
            device_id={"chan": me}, device_id_type=MESH,
        )

    if group > 1:
        sent(held.at[0 : (group - 1) * rows, :], send_sem).wait_send()

    @pl.when(slab < slabs - 1)
    def _():
        sent(raw.at[:, 0:HALO], hop_sem.at[0]).wait_send()

    @pl.when(slab > 0)
    def _():
        sent(raw.at[:, 0:HALO], hop_sem.at[1]).wait_send()

    others = sums.at[0 : n_chan - 1]
    everyone = pltpu.make_async_remote_copy(
        src_ref=others, dst_ref=others, send_sem=sum_send, recv_sem=sum_recv,
        device_id={"chan": me}, device_id_type=MESH,
    )
    everyone.wait_send()
    everyone.wait_recv()

    for b in range(group):
        tot = sums[b]
        for z in range(1, slabs):
            tot = tot + sums[z * group + b]
        tot = jnp.concatenate(
            [tot[:, i * rows : (i + 1) * rows] for i in range(fold)], axis=0
        )
        hi, mid, lo = (v.astype(F32) for v in split3(tot))
        none = jnp.zeros_like(hi)
        left_side = jnp.concatenate([hi, hi, mid, hi, lo, mid, none, none], axis=0)
        left_side = left_side.T.astype(BF16)
        r = slice(b * rows, (b + 1) * rows)
        out[r, :] = held[r, :] - jnp.dot(left_side, right_side, preferred_element_type=F32)


def per_device(cube, windows, mask):
    pix, ch = cube.shape
    n_chan = lax.axis_size("chan")
    total = ch * n_chan
    group = min(n_chan, max(4, HALO // ch))
    slab_ch = group * ch
    rows = pix // group
    wide = slab_ch + 2 * HALO
    fold = max(1, LANES // rows)
    vmem = pl.BlockSpec(memory_space=pltpu.VMEM)
    dma = pltpu.SemaphoreType.DMA
    return pl.pallas_call(
        functools.partial(kernel, n_chan, group, total),
        out_shape=jax.ShapeDtypeStruct((pix, ch), F32),
        in_specs=[
            pl.BlockSpec(memory_space=pltpu.SMEM),
            pl.BlockSpec(memory_space=pl.ANY),
            vmem, vmem, vmem,
        ],
        out_specs=vmem,
        scratch_shapes=[
            pltpu.VMEM((pix, ch), F32),
            pltpu.VMEM((rows, wide), F32),
            pltpu.VMEM((BLOCK, wide), F32),
            pltpu.VMEM((BLOCK, wide), F32),
            pltpu.VMEM((rows, slab_ch), BF16),
            pltpu.VMEM((rows, slab_ch), BF16),
            pltpu.VMEM((TERMS, slab_ch), F32),
            pltpu.VMEM((3 * TERMS, slab_ch), BF16),
            pltpu.VMEM((n_chan, TERMS // fold, rows * fold), F32),
            dma, dma, dma, dma((2,)),
            dma((CHUNKS, group)), dma((CHUNKS,)), dma((CHUNKS,)),
            dma, dma,
        ],
        compiler_params=pltpu.CompilerParams(collective_id=0, has_side_effects=True),
    )(
        windows, cube, mask.reshape(-1, LANES), mask.reshape(1, total),
        jnp.asarray(linearization()),
    )


def solution(mesh):
    placed = (P("pix", "chan"), P(), P())
    return jax.shard_map(
        per_device, mesh=mesh, in_specs=placed, out_specs=P("pix", "chan"), check_vma=False
    )
```

```python
import functools
import math

import jax
import jax.numpy as jnp
import numpy as np
from jax import lax
from jax.experimental import pallas as pl
from jax.experimental.pallas import tpu as pltpu
from jax.sharding import PartitionSpec as P

TERMS = 16
PASSES = 8
WMAX = 1024
HALO = 2 * WMAX
LANES = 128
BLOCK = 16
CHUNKS = 4
SPLIT = 2
TAIL = True
MESH = pl.DeviceIdType.MESH
F32 = jnp.float32
BF16 = jnp.bfloat16


def chunk_spans(rows):
    part = rows // CHUNKS
    sizes = [part] * CHUNKS
    if TAIL and part >= 16:
        sizes[-1:] = [part // 2, part // 2]
    starts = [sum(sizes[:i]) for i in range(len(sizes))]
    return list(zip(starts, sizes))


def linearization():
    def a(r):
        return math.comb(2 * r, r) / 2.0**r

    out = np.zeros((2 * TERMS - 1, TERMS, TERMS))
    for n in range(TERMS):
        for m in range(TERMS):
            for r in range(min(n, m) + 1):
                k = n + m - 2 * r
                out[k, n, m] = (
                    a(r) * a(n - r) * a(m - r) / a(n + m - r)
                    * (2 * k + 1) / (2 * n + 2 * m - 2 * r + 1)
                )
    return out.astype(np.float32)


def next_legendre(order, xvals, here, before):
    return ((2.0 * order + 1.0) * xvals * here - order * before) * (1.0 / (order + 1.0))


def split3(v):
    hi = v.astype(BF16)
    rest = v - hi.astype(F32)
    mid = rest.astype(BF16)
    lo = (rest - mid.astype(F32)).astype(BF16)
    return hi, mid, lo


def kernel(
    n_chan, group, total,
    windows, cube, mask_sq_hbm, mask_row_hbm, lin_hbm,
    left_out, right_out,
    mask_sq, mask_row, lin, raw, ping, pong, fit, table, w3, sums,
    load_sem, token, own_sem, send_sem, hop_sem, recv_sem, up_sem, down_sem, sum_send, sum_recv,
):
    pix, ch = cube.shape
    rows = raw.shape[0]
    slab_ch = group * ch
    tiles = slab_ch // LANES
    slabs = n_chan // group
    spans = chunk_spans(rows)
    me = lax.axis_index("chan")
    slab = me // group
    g = lax.rem(me, group)
    own_col = pl.multiple_of(HALO + g * ch, LANES)

    def peer(b):
        return {"chan": slab * group + b}

    own_rows = pl.multiple_of(g * rows, 8)
    barrier = pltpu.get_barrier_semaphore()

    def greet(device):
        pl.semaphore_signal(
            barrier, inc=1, device_id={"chan": device}, device_id_type=MESH
        )

    for k in range(1, group):
        greet(slab * group + lax.rem(g + k, group))

    @pl.when(slab > 0)
    def _():
        greet(me - group)

    @pl.when(slab < slabs - 1)
    def _():
        greet(me + group)

    loads = [
        pltpu.make_async_copy(mask_sq_hbm, mask_sq, load_sem.at[0]),
        pltpu.make_async_copy(mask_row_hbm, mask_row, load_sem.at[1]),
        pltpu.make_async_copy(lin_hbm, lin, load_sem.at[2]),
    ]
    own = pltpu.make_async_copy(
        cube.at[pl.ds(own_rows, rows), :], raw.at[:, pl.ds(own_col, ch)], own_sem
    )
    for copy in loads:
        copy.start()
    own.start()

    @pl.when(slab == 0)
    def _():
        raw[:, 0:HALO] = jnp.full((rows, HALO), jnp.inf, F32)

    @pl.when(slab == slabs - 1)
    def _():
        raw[:, HALO + slab_ch :] = jnp.full((rows, HALO), jnp.inf, F32)

    near = group - 1 + jnp.where(slab > 0, 1, 0) + jnp.where(slab < slabs - 1, 1, 0)
    pl.semaphore_wait(barrier, near)

    points = min(slabs, 3)

    def relay(point):
        for up in (True, False):
            place = slab if up else slabs - 1 - slab
            sem = token.at[0 if up else 1]
            to = me + group if up else me - group
            turn = (place == point) if point < points - 1 else (place >= point)

            @pl.when(turn)
            def _():
                if point > 0:
                    pl.semaphore_wait(sem, 1)

                @pl.when(place < slabs - 1)
                def _():
                    pl.semaphore_signal(
                        sem, inc=1, device_id={"chan": to}, device_id_type=MESH
                    )

    def chunk(c):
        return pl.ds(*spans[c])

    def slab_send(c, b):
        return pltpu.make_async_remote_copy(
            src_ref=cube.at[pl.ds(b * rows + spans[c][0], spans[c][1]), :],
            dst_ref=raw.at[chunk(c), pl.ds(own_col, ch)],
            send_sem=send_sem, recv_sem=recv_sem.at[c, g],
            device_id=peer(b), device_id_type=MESH,
        )

    def slab_recv(c, b):
        return pltpu.make_async_remote_copy(
            src_ref=cube.at[chunk(c), :],
            dst_ref=raw.at[chunk(c), pl.ds(HALO + b * ch, ch)],
            send_sem=send_sem, recv_sem=recv_sem.at[c, b],
            device_id=peer(b), device_id_type=MESH,
        )

    def hop(c, b, up, from_own):
        if up:
            col = b * ch - (slab_ch - HALO)
            sem, to = up_sem.at[c], me + group
        else:
            col = HALO + slab_ch + b * ch
            sem, to = down_sem.at[c], me - group
        if from_own:
            src = cube.at[pl.ds(pl.multiple_of(own_rows + spans[c][0], 8), spans[c][1]), :]
        else:
            src = raw.at[chunk(c), pl.ds(HALO + b * ch, ch)]
        return pltpu.make_async_remote_copy(
            src_ref=src, dst_ref=raw.at[chunk(c), pl.ds(col, ch)],
            send_sem=hop_sem.at[0 if up else 1], recv_sem=sem,
            device_id={"chan": to}, device_id_type=MESH,
        )

    def goes_up(b):
        return b * ch >= slab_ch - HALO

    def goes_down(b):
        return b * ch < HALO

    def own_hops(c):
        for b in range(group):
            if goes_up(b):
                @pl.when((g == b) & (slab < slabs - 1))
                def _():
                    hop(c, b, True, True).start()
            if goes_down(b):
                @pl.when((g == b) & (slab > 0))
                def _():
                    hop(c, b, False, True).start()

    def forward(c):
        for b in range(group):
            @pl.when(g != b)
            def _():
                slab_recv(c, b).wait_recv()
                if goes_up(b):
                    @pl.when(slab < slabs - 1)
                    def _():
                        hop(c, b, True, False).start()
                if goes_down(b):
                    @pl.when(slab > 0)
                    def _():
                        hop(c, b, False, False).start()

    def halo_wait(c):
        def arrived(col, sem):
            return pltpu.make_async_remote_copy(
                src_ref=raw.at[chunk(c), pl.ds(col, HALO)],
                dst_ref=raw.at[chunk(c), pl.ds(col, HALO)],
                send_sem=hop_sem.at[0], recv_sem=sem,
                device_id={"chan": me}, device_id_type=MESH,
            )

        @pl.when(slab > 0)
        def _():
            arrived(0, up_sem.at[c]).wait_recv()

        @pl.when(slab < slabs - 1)
        def _():
            arrived(HALO + slab_ch, down_sem.at[c]).wait_recv()

    for c in range(len(spans)):
        for b in range(group):
            @pl.when(g != b)
            def _():
                slab_send(c, b).start()
        own_hops(c)
    relay(0)
    for copy in loads:
        copy.wait()

    shape = mask_sq.shape
    index = lax.broadcasted_iota(jnp.int32, shape, 0) * shape[1] + lax.broadcasted_iota(
        jnp.int32, shape, 1
    )
    xvals = (2.0 * index.astype(F32) + 1.0) * (1.0 / total) - 1.0
    keep = mask_sq[...].astype(F32)
    here, before = jnp.ones_like(xvals), jnp.zeros_like(xvals)
    gram = jnp.zeros((TERMS, TERMS), F32)
    for k in range(2 * TERMS - 1):
        moment = jnp.sum(here * keep, axis=0, keepdims=True)
        moment = jnp.sum(moment, axis=1, keepdims=True)
        gram = gram + moment * lin[k]
        here, before = next_legendre(k, xvals, here, before), here

    row_id = lax.broadcasted_iota(jnp.int32, (TERMS, 2 * TERMS), 0)
    col_id = lax.broadcasted_iota(jnp.int32, (TERMS, 2 * TERMS), 1)
    eye = jnp.where(row_id + TERMS == col_id, 1.0, 0.0).astype(F32)
    aug = eye + jnp.concatenate([gram, jnp.zeros_like(gram)], axis=1)
    for p in range(TERMS):
        lead = aug[p : p + 1, :] / aug[p : p + 1, p : p + 1]
        aug = jnp.where(row_id == p, lead, aug - aug[:, p : p + 1] * lead)
    inverse = aug[:, TERMS:]

    forward(0)

    step = min(1024, slab_ch)
    base = slab * slab_ch
    for s in range(0, slab_ch, step):
        lane = lax.broadcasted_iota(jnp.int32, (1, step), 1)
        x_s = (2.0 * (base + s + lane).astype(F32) + 1.0) * (1.0 / total) - 1.0
        here, before = jnp.ones_like(x_s), jnp.zeros_like(x_s)
        for n in range(TERMS):
            table[n : n + 1, s : s + step] = here
            here, before = next_legendre(n, x_s, here, before), here
        keep_s = mask_row[:, pl.ds(pl.multiple_of(base + s, LANES), step)].astype(F32)
        hi, mid, lo = split3(table[:, s : s + step] * keep_s)
        w3[0:TERMS, s : s + step] = hi
        w3[TERMS : 2 * TERMS, s : s + step] = mid
        w3[2 * TERMS :, s : s + step] = lo

    forward(1)

    own.wait()
    edge = HALO // LANES

    def snip(start, block):
        r = pl.ds(start, block)
        lane = lax.broadcasted_iota(jnp.int32, (block, LANES), 1)

        def at(ref, t):
            return ref[0:block, (t + edge) * LANES : (t + edge + 1) * LANES]

        def put(ref, t, v):
            ref[0:block, (t + edge) * LANES : (t + edge + 1) * LANES] = v

        def first(t):
            return raw[r, (t + edge) * LANES : (t + edge + 1) * LANES]

        far = WMAX // LANES
        for t in range(-far, tiles + far):
            put(ping, t, jnp.minimum(first(t), 0.5 * (first(t - far) + first(t + far))))
        src, dst = ping, pong
        for k in range(1, PASSES):
            bound = max(LANES, WMAX >> k)
            b = bound // LANES
            d = bound - windows[k]
            back = lax.rem(LANES - d, LANES)
            low_here = lane < LANES - d
            high_here = lane >= d
            reach = 0 if k == PASSES - 1 else b
            left = {}
            right = {}
            for t in range(-reach, tiles + reach):
                for u in (t - b, t - b + 1):
                    if u not in left:
                        left[u] = pltpu.roll(at(src, u), back, 1)
                for u in (t + b - 1, t + b):
                    if u not in right:
                        right[u] = pltpu.roll(at(src, u), d, 1)
                lower = jnp.where(low_here, left[t - b], left[t - b + 1])
                upper = jnp.where(high_here, right[t + b], right[t + b - 1])
                v = jnp.minimum(at(src, t), 0.5 * (lower + upper))
                if k < PASSES - 1:
                    put(dst, t, v)
                else:
                    cols = slice(t * LANES, (t + 1) * LANES)
                    fit[r, cols] = v
            src, dst = dst, src

    def process(c):
        halo_wait(c)
        first_row, part = spans[c]
        block = min(BLOCK, part)
        if part == block:
            snip(first_row, block)
        else:
            def body(i, carry):
                snip(pl.multiple_of(first_row + i * block, 8), block)
                return carry
            lax.fori_loop(0, part // block, body, 0)

    for c in range(len(spans)):
        if c + 2 < len(spans):
            forward(c + 2)
        process(c)
        if c in (0, 1) and c + 1 < points:
            relay(c + 1)

    dims = (((1,), (1,)), ((), ()))
    whole = fit[...]
    fit_hi = whole.astype(BF16)
    fit_lo = (whole - fit_hi.astype(F32)).astype(BF16)
    rhs3 = lax.dot_general(w3[...], fit_hi, dims, preferred_element_type=F32)
    rhs3 = rhs3 + lax.dot_general(w3[...], fit_lo, dims, preferred_element_type=F32)
    rhs = rhs3[0:TERMS] + (rhs3[TERMS : 2 * TERMS] + rhs3[2 * TERMS :])
    fold = sums.shape[2] // rows
    high = TERMS // fold
    packed = jnp.concatenate([rhs[i * high : (i + 1) * high] for i in range(fold)], axis=1)
    sums[me] = packed

    def sum_copy(k):
        return pltpu.make_async_remote_copy(
            src_ref=sums.at[me], dst_ref=sums.at[me],
            send_sem=sum_send, recv_sem=sum_recv,
            device_id={"chan": lax.rem(me + k, n_chan)}, device_id_type=MESH,
        )

    for k in range(1, n_chan):
        sum_copy(k).start()

    t_own = table[:, pl.ds(pl.multiple_of(g * ch, LANES), ch)]
    shaped = jnp.zeros_like(t_own)
    for m in range(TERMS):
        shaped = shaped + inverse[:, m : m + 1] * t_own[m : m + 1, :]
    a_hi, a_mid, a_lo = split3(shaped)
    zero = jnp.zeros_like(a_hi)
    right_out[...] = jnp.concatenate(
        [a_hi, a_mid, a_hi, a_lo, a_hi, a_mid, zero, zero], axis=0
    )

    def sent(ref, sem):
        return pltpu.make_async_remote_copy(
            src_ref=ref, dst_ref=ref, send_sem=sem, recv_sem=own_sem,
            device_id={"chan": me}, device_id_type=MESH,
        )

    if group > 1:
        sent(cube.at[0 : (group - 1) * rows, :], send_sem).wait_send()

    @pl.when(slab < slabs - 1)
    def _():
        sent(raw.at[:, 0:HALO], hop_sem.at[0]).wait_send()

    @pl.when(slab > 0)
    def _():
        sent(raw.at[:, 0:HALO], hop_sem.at[1]).wait_send()

    others = sums.at[0 : n_chan - 1]
    everyone = pltpu.make_async_remote_copy(
        src_ref=others, dst_ref=others, send_sem=sum_send, recv_sem=sum_recv,
        device_id={"chan": me}, device_id_type=MESH,
    )
    everyone.wait_send()
    everyone.wait_recv()

    for b in range(group):
        tot = sums[b]
        for z in range(1, slabs):
            tot = tot + sums[z * group + b]
        tot = jnp.concatenate(
            [tot[:, i * rows : (i + 1) * rows] for i in range(fold)], axis=0
        )
        hi, mid, lo = (v.astype(F32) for v in split3(tot))
        none = jnp.zeros_like(hi)
        left_side = jnp.concatenate([hi, hi, mid, hi, lo, mid, none, none], axis=0)
        left_out[b * rows : (b + 1) * rows, :] = left_side.T.astype(BF16)


def subtract(cube, left, right, out):
    out[...] = cube[...] - jnp.dot(left[...], right[...], preferred_element_type=F32)


def per_device(cube, windows, mask):
    pix, ch = cube.shape
    n_chan = lax.axis_size("chan")
    total = ch * n_chan
    group = min(n_chan, max(4, HALO // ch))
    slab_ch = group * ch
    rows = pix // group
    wide = slab_ch + 2 * HALO
    fold = max(1, LANES // rows)
    vmem = pl.BlockSpec(memory_space=pltpu.VMEM)
    hbm = pl.BlockSpec(memory_space=pl.ANY)
    dma = pltpu.SemaphoreType.DMA
    chunks = len(chunk_spans(rows))
    lin = jnp.asarray(linearization())
    depth = 8 * TERMS
    left, right = pl.pallas_call(
        functools.partial(kernel, n_chan, group, total),
        out_shape=(
            jax.ShapeDtypeStruct((pix, depth), BF16),
            jax.ShapeDtypeStruct((depth, ch), BF16),
        ),
        in_specs=[pl.BlockSpec(memory_space=pltpu.SMEM), hbm, hbm, hbm, hbm],
        out_specs=(vmem, vmem),
        scratch_shapes=[
            pltpu.VMEM((total // LANES, LANES), jnp.int32),
            pltpu.VMEM((1, total), jnp.int32),
            pltpu.VMEM(lin.shape, F32),
            pltpu.VMEM((rows, wide), F32),
            pltpu.VMEM((BLOCK, wide), F32),
            pltpu.VMEM((BLOCK, wide), F32),
            pltpu.VMEM((rows, slab_ch), F32),
            pltpu.VMEM((TERMS, slab_ch), F32),
            pltpu.VMEM((3 * TERMS, slab_ch), BF16),
            pltpu.VMEM((n_chan, TERMS // fold, rows * fold), F32),
            dma((3,)), pltpu.SemaphoreType.REGULAR((2,)), dma, dma, dma((2,)),
            dma((chunks, group)), dma((chunks,)), dma((chunks,)),
            dma, dma,
        ],
        compiler_params=pltpu.CompilerParams(
            collective_id=0, has_side_effects=True
        ),
    )(windows, cube, mask.reshape(-1, LANES), mask.reshape(1, total), lin)
    step = max(pix // SPLIT, 16)
    return pl.pallas_call(
        subtract,
        grid=(pix // step,),
        out_shape=jax.ShapeDtypeStruct((pix, ch), F32),
        in_specs=[
            pl.BlockSpec((step, ch), lambda i: (i, 0)),
            pl.BlockSpec((step, depth), lambda i: (i, 0)),
            pl.BlockSpec((depth, ch), lambda i: (0, 0)),
        ],
        out_specs=pl.BlockSpec((step, ch), lambda i: (i, 0)),
    )(cube, left, right)


def solution(mesh):
    placed = (P("pix", "chan"), P(), P())
    return jax.shard_map(
        per_device, mesh=mesh, in_specs=placed, out_specs=P("pix", "chan"), check_vma=False
    )
```

```python
import functools
import math

import jax
import jax.numpy as jnp
import numpy as np
from jax import lax
from jax.experimental import pallas as pl
from jax.experimental.pallas import tpu as pltpu
from jax.sharding import PartitionSpec as P

TERMS = 16
PASSES = 8
WMAX = 1024
HALO = 2 * WMAX
LANES = 128
BLOCK = 16
CHUNKS = 4
SPLIT = 2
TAIL = True
MESH = pl.DeviceIdType.MESH
F32 = jnp.float32
BF16 = jnp.bfloat16


def chunk_spans(rows):
    part = rows // CHUNKS
    sizes = [part] * CHUNKS
    if TAIL and part >= 16:
        sizes[-1:] = [part // 2, part // 2]
    starts = [sum(sizes[:i]) for i in range(len(sizes))]
    return list(zip(starts, sizes))


def linearization():
    def a(r):
        return math.comb(2 * r, r) / 2.0**r

    out = np.zeros((2 * TERMS - 1, TERMS, TERMS))
    for n in range(TERMS):
        for m in range(TERMS):
            for r in range(min(n, m) + 1):
                k = n + m - 2 * r
                out[k, n, m] = (
                    a(r) * a(n - r) * a(m - r) / a(n + m - r)
                    * (2 * k + 1) / (2 * n + 2 * m - 2 * r + 1)
                )
    return out.astype(np.float32)


def next_legendre(order, xvals, here, before):
    return ((2.0 * order + 1.0) * xvals * here - order * before) * (1.0 / (order + 1.0))


def split3(v):
    hi = v.astype(BF16)
    rest = v - hi.astype(F32)
    mid = rest.astype(BF16)
    lo = (rest - mid.astype(F32)).astype(BF16)
    return hi, mid, lo


def kernel(
    n_chan, group, total,
    windows_hbm, cube, mask_sq_hbm, mask_row_hbm, lin_hbm,
    left_out, right_hbm,
    windows, right_out, mask_sq, mask_row, lin, raw, ping, pong, fit, table, w3, sums,
    load_sem, right_sem, token, own_sem, send_sem, hop_sem, recv_sem, up_sem, down_sem, sum_send, sum_recv,
):
    pix, ch = cube.shape
    rows = raw.shape[0]
    slab_ch = group * ch
    tiles = slab_ch // LANES
    slabs = n_chan // group
    spans = chunk_spans(rows)
    me = lax.axis_index("chan")
    slab = me // group
    g = lax.rem(me, group)
    own_col = pl.multiple_of(HALO + g * ch, LANES)

    def peer(b):
        return {"chan": slab * group + b}

    own_rows = pl.multiple_of(g * rows, 8)
    barrier = pltpu.get_barrier_semaphore()

    def greet(device):
        pl.semaphore_signal(
            barrier, inc=1, device_id={"chan": device}, device_id_type=MESH
        )

    for k in range(1, group):
        greet(slab * group + lax.rem(g + k, group))

    @pl.when(slab > 0)
    def _():
        greet(me - group)

    @pl.when(slab < slabs - 1)
    def _():
        greet(me + group)

    loads = [
        pltpu.make_async_copy(mask_sq_hbm, mask_sq, load_sem.at[0]),
        pltpu.make_async_copy(mask_row_hbm, mask_row, load_sem.at[1]),
        pltpu.make_async_copy(lin_hbm, lin, load_sem.at[2]),
        pltpu.make_async_copy(windows_hbm, windows, load_sem.at[3]),
    ]
    own = pltpu.make_async_copy(
        cube.at[pl.ds(own_rows, rows), :], raw.at[:, pl.ds(own_col, ch)], own_sem
    )
    for copy in loads:
        copy.start()
    own.start()

    @pl.when(slab == 0)
    def _():
        raw[:, 0:HALO] = jnp.full((rows, HALO), jnp.inf, F32)

    @pl.when(slab == slabs - 1)
    def _():
        raw[:, HALO + slab_ch :] = jnp.full((rows, HALO), jnp.inf, F32)

    near = group - 1 + jnp.where(slab > 0, 1, 0) + jnp.where(slab < slabs - 1, 1, 0)
    pl.semaphore_wait(barrier, near)

    points = min(slabs, 3)

    def relay(point):
        for up in (True, False):
            place = slab if up else slabs - 1 - slab
            sem = token.at[0 if up else 1]
            to = me + group if up else me - group
            turn = (place == point) if point < points - 1 else (place >= point)

            @pl.when(turn)
            def _():
                if point > 0:
                    pl.semaphore_wait(sem, 1)

                @pl.when(place < slabs - 1)
                def _():
                    pl.semaphore_signal(
                        sem, inc=1, device_id={"chan": to}, device_id_type=MESH
                    )

    def chunk(c):
        return pl.ds(*spans[c])

    def slab_send(c, b):
        return pltpu.make_async_remote_copy(
            src_ref=cube.at[pl.ds(b * rows + spans[c][0], spans[c][1]), :],
            dst_ref=raw.at[chunk(c), pl.ds(own_col, ch)],
            send_sem=send_sem, recv_sem=recv_sem.at[c, g],
            device_id=peer(b), device_id_type=MESH,
        )

    def slab_recv(c, b):
        return pltpu.make_async_remote_copy(
            src_ref=cube.at[chunk(c), :],
            dst_ref=raw.at[chunk(c), pl.ds(HALO + b * ch, ch)],
            send_sem=send_sem, recv_sem=recv_sem.at[c, b],
            device_id=peer(b), device_id_type=MESH,
        )

    def hop(c, b, up, from_own):
        if up:
            col = b * ch - (slab_ch - HALO)
            sem, to = up_sem.at[c], me + group
        else:
            col = HALO + slab_ch + b * ch
            sem, to = down_sem.at[c], me - group
        if from_own:
            src = cube.at[pl.ds(pl.multiple_of(own_rows + spans[c][0], 8), spans[c][1]), :]
        else:
            src = raw.at[chunk(c), pl.ds(HALO + b * ch, ch)]
        return pltpu.make_async_remote_copy(
            src_ref=src, dst_ref=raw.at[chunk(c), pl.ds(col, ch)],
            send_sem=hop_sem.at[0 if up else 1], recv_sem=sem,
            device_id={"chan": to}, device_id_type=MESH,
        )

    def goes_up(b):
        return b * ch >= slab_ch - HALO

    def goes_down(b):
        return b * ch < HALO

    def own_hops(c):
        for b in range(group):
            if goes_up(b):
                @pl.when((g == b) & (slab < slabs - 1))
                def _():
                    hop(c, b, True, True).start()
            if goes_down(b):
                @pl.when((g == b) & (slab > 0))
                def _():
                    hop(c, b, False, True).start()

    def forward(c):
        for b in range(group):
            @pl.when(g != b)
            def _():
                slab_recv(c, b).wait_recv()
                if goes_up(b):
                    @pl.when(slab < slabs - 1)
                    def _():
                        hop(c, b, True, False).start()
                if goes_down(b):
                    @pl.when(slab > 0)
                    def _():
                        hop(c, b, False, False).start()

    def halo_wait(c):
        def arrived(col, sem):
            return pltpu.make_async_remote_copy(
                src_ref=raw.at[chunk(c), pl.ds(col, HALO)],
                dst_ref=raw.at[chunk(c), pl.ds(col, HALO)],
                send_sem=hop_sem.at[0], recv_sem=sem,
                device_id={"chan": me}, device_id_type=MESH,
            )

        @pl.when(slab > 0)
        def _():
            arrived(0, up_sem.at[c]).wait_recv()

        @pl.when(slab < slabs - 1)
        def _():
            arrived(HALO + slab_ch, down_sem.at[c]).wait_recv()

    for c in range(len(spans)):
        for b in range(group):
            @pl.when(g != b)
            def _():
                slab_send(c, b).start()
        own_hops(c)
    relay(0)
    for copy in loads:
        copy.wait()

    shape = mask_sq.shape
    index = lax.broadcasted_iota(jnp.int32, shape, 0) * shape[1] + lax.broadcasted_iota(
        jnp.int32, shape, 1
    )
    xvals = (2.0 * index.astype(F32) + 1.0) * (1.0 / total) - 1.0
    keep = mask_sq[...].astype(F32)
    here, before = jnp.ones_like(xvals), jnp.zeros_like(xvals)
    gram = jnp.zeros((TERMS, TERMS), F32)
    for k in range(2 * TERMS - 1):
        moment = jnp.sum(here * keep, axis=0, keepdims=True)
        moment = jnp.sum(moment, axis=1, keepdims=True)
        gram = gram + moment * lin[k]
        here, before = next_legendre(k, xvals, here, before), here

    row_id = lax.broadcasted_iota(jnp.int32, (TERMS, 2 * TERMS), 0)
    col_id = lax.broadcasted_iota(jnp.int32, (TERMS, 2 * TERMS), 1)
    eye = jnp.where(row_id + TERMS == col_id, 1.0, 0.0).astype(F32)
    aug = eye + jnp.concatenate([gram, jnp.zeros_like(gram)], axis=1)
    for p in range(TERMS):
        lead = aug[p : p + 1, :] / aug[p : p + 1, p : p + 1]
        aug = jnp.where(row_id == p, lead, aug - aug[:, p : p + 1] * lead)
    inverse = aug[:, TERMS:]

    forward(0)

    step = min(1024, slab_ch)
    base = slab * slab_ch
    for s in range(0, slab_ch, step):
        lane = lax.broadcasted_iota(jnp.int32, (1, step), 1)
        x_s = (2.0 * (base + s + lane).astype(F32) + 1.0) * (1.0 / total) - 1.0
        here, before = jnp.ones_like(x_s), jnp.zeros_like(x_s)
        for n in range(TERMS):
            table[n : n + 1, s : s + step] = here
            here, before = next_legendre(n, x_s, here, before), here
        keep_s = mask_row[:, pl.ds(pl.multiple_of(base + s, LANES), step)].astype(F32)
        hi, mid, lo = split3(table[:, s : s + step] * keep_s)
        w3[0:TERMS, s : s + step] = hi
        w3[TERMS : 2 * TERMS, s : s + step] = mid
        w3[2 * TERMS :, s : s + step] = lo

    forward(1)

    own.wait()
    edge = HALO // LANES

    def snip(start, block):
        r = pl.ds(start, block)
        lane = lax.broadcasted_iota(jnp.int32, (block, LANES), 1)

        def at(ref, t):
            return ref[0:block, (t + edge) * LANES : (t + edge + 1) * LANES]

        def put(ref, t, v):
            ref[0:block, (t + edge) * LANES : (t + edge + 1) * LANES] = v

        def first(t):
            return raw[r, (t + edge) * LANES : (t + edge + 1) * LANES]

        far = WMAX // LANES
        for t in range(-far, tiles + far):
            put(ping, t, jnp.minimum(first(t), 0.5 * (first(t - far) + first(t + far))))
        src, dst = ping, pong
        for k in range(1, PASSES):
            bound = max(LANES, WMAX >> k)
            b = bound // LANES
            d = bound - windows[k]
            back = lax.rem(LANES - d, LANES)
            low_here = lane < LANES - d
            high_here = lane >= d
            reach = 0 if k == PASSES - 1 else b
            left = {}
            right = {}
            for t in range(-reach, tiles + reach):
                for u in (t - b, t - b + 1):
                    if u not in left:
                        left[u] = pltpu.roll(at(src, u), back, 1)
                for u in (t + b - 1, t + b):
                    if u not in right:
                        right[u] = pltpu.roll(at(src, u), d, 1)
                lower = jnp.where(low_here, left[t - b], left[t - b + 1])
                upper = jnp.where(high_here, right[t + b], right[t + b - 1])
                v = jnp.minimum(at(src, t), 0.5 * (lower + upper))
                if k < PASSES - 1:
                    put(dst, t, v)
                else:
                    cols = slice(t * LANES, (t + 1) * LANES)
                    fit[r, cols] = v
            src, dst = dst, src

    def process(c):
        halo_wait(c)
        first_row, part = spans[c]
        block = min(BLOCK, part)
        if part == block:
            snip(first_row, block)
        else:
            def body(i, carry):
                snip(pl.multiple_of(first_row + i * block, 8), block)
                return carry
            lax.fori_loop(0, part // block, body, 0)

    dims = (((1,), (1,)), ((), ()))

    def products(lo, hi):
        whole = fit[lo:hi, :]
        fit_hi = whole.astype(BF16)
        fit_lo = (whole - fit_hi.astype(F32)).astype(BF16)
        rhs3 = lax.dot_general(w3[...], fit_hi, dims, preferred_element_type=F32)
        rhs3 = rhs3 + lax.dot_general(w3[...], fit_lo, dims, preferred_element_type=F32)
        return rhs3[0:TERMS] + (rhs3[TERMS : 2 * TERMS] + rhs3[2 * TERMS :])

    cut = rows * (CHUNKS - 1) // CHUNKS
    for c in range(len(spans)):
        if c + 2 < len(spans):
            forward(c + 2)
        process(c)
        if c in (0, 1) and c + 1 < points:
            relay(c + 1)
        if sum(spans[c]) == cut:
            early = products(0, cut)
    rhs = jnp.concatenate([early, products(cut, rows)], axis=1)
    fold = sums.shape[2] // rows
    high = TERMS // fold
    packed = jnp.concatenate([rhs[i * high : (i + 1) * high] for i in range(fold)], axis=1)
    sums[me] = packed

    def sum_copy(k):
        return pltpu.make_async_remote_copy(
            src_ref=sums.at[me], dst_ref=sums.at[me],
            send_sem=sum_send, recv_sem=sum_recv,
            device_id={"chan": lax.rem(me + k, n_chan)}, device_id_type=MESH,
        )

    for k in range(1, n_chan):
        sum_copy(k).start()

    t_own = table[:, pl.ds(pl.multiple_of(g * ch, LANES), ch)]
    shaped = jnp.zeros_like(t_own)
    for m in range(TERMS):
        shaped = shaped + inverse[:, m : m + 1] * t_own[m : m + 1, :]
    a_hi, a_mid, a_lo = split3(shaped)
    zero = jnp.zeros_like(a_hi)
    right_out[...] = jnp.concatenate(
        [a_hi, a_mid, a_hi, a_lo, a_hi, a_mid, zero, zero], axis=0
    )
    right_copy = pltpu.make_async_copy(right_out, right_hbm, right_sem)
    right_copy.start()

    def sent(ref, sem):
        return pltpu.make_async_remote_copy(
            src_ref=ref, dst_ref=ref, send_sem=sem, recv_sem=own_sem,
            device_id={"chan": me}, device_id_type=MESH,
        )

    if group > 1:
        sent(cube.at[0 : (group - 1) * rows, :], send_sem).wait_send()

    @pl.when(slab < slabs - 1)
    def _():
        sent(raw.at[:, 0:HALO], hop_sem.at[0]).wait_send()

    @pl.when(slab > 0)
    def _():
        sent(raw.at[:, 0:HALO], hop_sem.at[1]).wait_send()

    others = sums.at[0 : n_chan - 1]
    everyone = pltpu.make_async_remote_copy(
        src_ref=others, dst_ref=others, send_sem=sum_send, recv_sem=sum_recv,
        device_id={"chan": me}, device_id_type=MESH,
    )
    everyone.wait_send()
    everyone.wait_recv()
    right_copy.wait()

    for b in range(group):
        tot = sums[b]
        for z in range(1, slabs):
            tot = tot + sums[z * group + b]
        tot = jnp.concatenate(
            [tot[:, i * rows : (i + 1) * rows] for i in range(fold)], axis=0
        )
        hi, mid, lo = (v.astype(F32) for v in split3(tot))
        none = jnp.zeros_like(hi)
        left_side = jnp.concatenate([hi, hi, mid, hi, lo, mid, none, none], axis=0)
        left_out[b * rows : (b + 1) * rows, :] = left_side.T.astype(BF16)


def subtract(cube, left, right, out):
    out[...] = cube[...] - jnp.dot(left[...], right[...], preferred_element_type=F32)


def per_device(cube, windows, mask):
    pix, ch = cube.shape
    n_chan = lax.axis_size("chan")
    total = ch * n_chan
    group = min(n_chan, max(4, HALO // ch))
    slab_ch = group * ch
    rows = pix // group
    wide = slab_ch + 2 * HALO
    fold = max(1, LANES // rows)
    vmem = pl.BlockSpec(memory_space=pltpu.VMEM)
    hbm = pl.BlockSpec(memory_space=pl.ANY)
    dma = pltpu.SemaphoreType.DMA
    chunks = len(chunk_spans(rows))
    lin = jnp.asarray(linearization())
    depth = 8 * TERMS
    left, right = pl.pallas_call(
        functools.partial(kernel, n_chan, group, total),
        out_shape=(
            jax.ShapeDtypeStruct((pix, depth), BF16),
            jax.ShapeDtypeStruct((depth, ch), BF16),
        ),
        in_specs=[hbm, hbm, hbm, hbm, hbm],
        out_specs=(vmem, hbm),
        scratch_shapes=[
            pltpu.SMEM(windows.shape, jnp.int32),
            pltpu.VMEM((depth, ch), BF16),
            pltpu.VMEM((total // LANES, LANES), jnp.int32),
            pltpu.VMEM((1, total), jnp.int32),
            pltpu.VMEM(lin.shape, F32),
            pltpu.VMEM((rows, wide), F32),
            pltpu.VMEM((BLOCK, wide), F32),
            pltpu.VMEM((BLOCK, wide), F32),
            pltpu.VMEM((rows, slab_ch), F32),
            pltpu.VMEM((TERMS, slab_ch), F32),
            pltpu.VMEM((3 * TERMS, slab_ch), BF16),
            pltpu.VMEM((n_chan, TERMS // fold, rows * fold), F32),
            dma((4,)), dma, pltpu.SemaphoreType.REGULAR((2,)), dma, dma, dma((2,)),
            dma((chunks, group)), dma((chunks,)), dma((chunks,)),
            dma, dma,
        ],
        compiler_params=pltpu.CompilerParams(
            collective_id=0, has_side_effects=True
        ),
    )(windows, cube, mask.reshape(-1, LANES), mask.reshape(1, total), lin)
    step = max(pix // SPLIT, 16)
    return pl.pallas_call(
        subtract,
        grid=(pix // step,),
        out_shape=jax.ShapeDtypeStruct((pix, ch), F32),
        in_specs=[
            pl.BlockSpec((step, ch), lambda i: (i, 0)),
            pl.BlockSpec((step, depth), lambda i: (i, 0)),
            pl.BlockSpec((depth, ch), lambda i: (0, 0)),
        ],
        out_specs=pl.BlockSpec((step, ch), lambda i: (i, 0)),
    )(cube, left, right)


def solution(mesh):
    placed = (P("pix", "chan"), P(), P())
    return jax.shard_map(
        per_device, mesh=mesh, in_specs=placed, out_specs=P("pix", "chan"), check_vma=False
    )
```
